256 devices in a mesh: blk: 32 (over z, y_hi, core), rep: 8 (over x, y_lo).
Axes of the slice: x: 4, y: 4 (y_hi: 2, y_lo: 2; y = y_hi * 2 + y_lo), z: 8, core: 2. Of those that a mesh axis runs over, the one named last changes fastest.
Arguments:
- features: bfloat16 [65536, 256], P(('blk', 'rep')), may hold values from -6 to 6
- aggregated: bfloat16 [65536, 256], P(('blk', 'rep')), may hold values from -6 to 6
- out_grad: bfloat16 [65536, 256], P(('blk', 'rep')), may hold values from -6 to 6
- w_self: bfloat16 [256, 256], replicated, may hold values from -0.375 to 0.375
- w_neigh: bfloat16 [256, 256], replicated, may hold values from -0.375 to 0.375
- tiles: bfloat16 [32, 32, 8, 128, 128], P('blk'), may hold values from -0.046875 to 0.046875
- tile_rows: int32 [32, 32, 8], P('blk'), may hold values from 0 to 15
- tile_cols: int32 [32, 32, 8], P('blk'), may hold values from 0 to 15
- tile_counts: int32 [32, 32], P('blk'), may hold values from 0 to 8, as said below
Outputs:
- feature_grad: float32 [65536, 256], P(('blk', 'rep'))
- self_grad: float32 [256, 256], replicated
- neigh_grad: float32 [256, 256], replicated
The draws below stay inside these ranges and needn't reach their ends.
Inputs may be any that keep to these rules, and one draw needn't show every extreme that they name: `tile_counts`: at most 8; some pair of blocks uses all 8 slots; tiles, rows and columns of slots beyond the count carry no meaning.
All inputs are finite; a program needn't handle non-finite values.
Results may differ from the reference program's by a relative error of at most 0.00082.
Values may be sent and summed in bfloat16 or wider, within the bound.
No kernel may reach another device: no remote copies, remote signals or barrier semaphores. Data moves between devices by JAX's collectives and lax.ppermute only.
A program may use at most 64 MiB of HBM per device.

```python
import jax
import jax.numpy as jnp
from jax import lax

F = 256
TILE = 128
TB = 16
SLOTS = 8
VERTS = 65536
N_BLK = 32


def draw_tile_counts(key, part):
    inner = jax.random.fold_in(key, 11)
    first_key, second_key = jax.random.split(inner)
    base = jax.random.randint(first_key, (N_BLK, N_BLK), SLOTS // 2, SLOTS + 1)
    ceiling = SLOTS - jnp.arange(N_BLK, dtype=jnp.int32) * (SLOTS // 2) // N_BLK
    counts = jnp.minimum(base, ceiling[:, None])
    column = jax.random.randint(second_key, (), 0, N_BLK)
    counts = counts.at[0, column].set(SLOTS)
    return counts.astype(jnp.int32)


def place_ends(result, own_key, low, largest):
    spot = [jax.random.randint(jax.random.fold_in(own_key, axis), (), 0, length) for axis, length in enumerate(result.shape)]
    longest = result.shape.index(max(result.shape))
    next_to = spot[:longest] + [(spot[longest] + 1) % result.shape[longest]] + spot[longest + 1:]
    return result.at[tuple(spot)].set(low).at[tuple(next_to)].set(largest)


def shard_levels(own_key, extent, cuts, low, top_value):
    factor_of, own = 1.0, jax.random.fold_in(own_key, 6)
    for dim, shards_of in cuts:
        draws = jnp.exp(jax.random.uniform(jax.random.fold_in(own, dim), (shards_of,), jnp.float32, low / len(cuts), top_value / len(cuts)))
        factor_of = factor_of * jnp.repeat(draws, extent[dim] // shards_of).reshape([-1 if axis == dim else 1 for axis in range(len(extent))])
    return factor_of


def scatter_about(stream_key, dims, deviation, reach, cuts=(), held_as=jnp.bfloat16):
    drawn = jax.random.normal(stream_key, dims, jnp.float32) * deviation
    if len(cuts) > 0:
        drawn = shard_levels(stream_key, dims, cuts, -0.22, 0.18) * drawn
    return jnp.clip(drawn, min=-reach, max=reach).astype(held_as)


def setup_inputs(seed: int = 0) -> dict:
    arg_keys = jax.random.split(jax.random.key(seed), 10)
    return {
        "features": scatter_about(arg_keys[0], (VERTS, F), 1.0, 6.0, ((0, 256),)),
        "aggregated": scatter_about(arg_keys[1], (VERTS, F), 1.0, 6.0, ((0, 256),)),
        "out_grad": scatter_about(arg_keys[2], (VERTS, F), 1.0, 6.0, ((0, 256),)),
        "w_self": scatter_about(arg_keys[3], (F, F), F ** -0.5, 0.375),
        "w_neigh": scatter_about(arg_keys[4], (F, F), F ** -0.5, 0.375),
        "tiles": scatter_about(arg_keys[5], (N_BLK, N_BLK, SLOTS, TILE, TILE), (TILE * SLOTS * N_BLK // 2) ** -0.5, 0.046875, ((0, 32),)),
        "tile_rows": place_ends(jax.random.randint(arg_keys[6], (N_BLK, N_BLK, SLOTS), 0, TB), jax.random.fold_in(arg_keys[6], 1), 0, TB - 1).astype(jnp.int32),
        "tile_cols": place_ends(jax.random.randint(arg_keys[7], (N_BLK, N_BLK, SLOTS), 0, TB), jax.random.fold_in(arg_keys[7], 1), 0, TB - 1).astype(jnp.int32),
        "tile_counts": draw_tile_counts(jax.random.fold_in(arg_keys[9], 71), 0),
    }


def reference(features, aggregated, out_grad, w_self, w_neigh, tiles, tile_rows, tile_cols, tile_counts):
    message = jnp.dot(out_grad, w_neigh.T, preferred_element_type=jnp.float32).astype(jnp.bfloat16)
    pieces_all = message.reshape(N_BLK * TB, TILE, F)

    def one_block(block_index):
        blocks = tiles[block_index].reshape(N_BLK * SLOTS, TILE, TILE).astype(jnp.float32)
        index = (jnp.arange(N_BLK, dtype=jnp.int32)[:, None] * TB + tile_cols[block_index]).reshape(-1).astype(jnp.int32)
        pieces = pieces_all[index].astype(jnp.float32)
        products = jnp.einsum("kpq,kqf->kpf", blocks, pieces)
        live = (jnp.arange(SLOTS, dtype=jnp.int32)[None, :] < tile_counts[block_index][:, None]).reshape(-1)
        products = jnp.where(live[:, None, None], products, jnp.zeros_like(products))
        start = jnp.zeros((TB, TILE, F), products.dtype)
        return start.at[tile_rows[block_index].reshape(-1)].add(products)

    spread = lax.map(one_block, jnp.arange(N_BLK, dtype=jnp.int32)).reshape(N_BLK * TB * TILE, F)
    feature_grad = jnp.dot(out_grad, w_self.T, preferred_element_type=jnp.float32) + spread
    scale = VERTS ** -0.5
    contract = (((0,), (0,)), ((), ()))
    self_grad = lax.dot_general(features, out_grad, contract, preferred_element_type=jnp.float32) * scale
    neigh_grad = lax.dot_general(aggregated, out_grad, contract, preferred_element_type=jnp.float32) * scale
    return (feature_grad, self_grad, neigh_grad)
```

```python
import functools

import jax
import jax.numpy as jnp
from jax import lax
from jax.experimental import pallas as pl
from jax.experimental.pallas import tpu as pltpu
from jax.sharding import PartitionSpec as P

PLANE = 4
BOTH = ("blk", "rep")


def plane_exchange(x, groups):
    return lax.all_to_all(x, BOTH, 0, 0, axis_index_groups=groups, tiled=True)


def spread_kernel(
    pieces_total, slots, ids, rows, cols, tiles, *rest
):
    pieces = rest[:pieces_total]
    out = rest[pieces_total]
    held, tile_buf, acc, piece_sems, tile_sems = rest[pieces_total + 1 :]
    tiles_side = out.shape[0]
    blocks_total = ids.shape[0]
    begun = []
    at = 0
    for index, piece in enumerate(pieces):
        length = piece.shape[0]
        begun.append(
            pltpu.make_async_copy(piece, held.at[pl.ds(at, length)], piece_sems.at[index])
        )
        at += length

    def tile_copy(n):
        return pltpu.make_async_copy(tiles.at[ids[n]], tile_buf.at[n], tile_sems.at[n])

    for copy in begun:
        copy.start()

    @pl.loop(0, blocks_total)
    def _(n):
        tile_copy(n).start()

    acc[...] = jnp.zeros_like(acc)
    for copy in begun:
        copy.wait()

    @pl.loop(0, blocks_total)
    def _(n):
        tile_copy(n).wait()
        base = ids[n] * slots
        products = [
            lax.dot_general(
                held[n, cols[base + k]],
                tile_buf[n, k],
                (((1,), (1,)), ((), ())),
                preferred_element_type=jnp.float32,
            )
            for k in range(slots)
        ]
        for k in range(slots):
            row = rows[base + k]
            acc[row] = acc[row] + products[k]

    out[...] = acc[:tiles_side]


def spread_over(pieces, ids, rows, cols, tiles, tiles_side):
    blocks_total, slots, side, _ = tiles.shape
    features = pieces[0].shape[-2]
    held = (blocks_total, *pieces[0].shape[1:])
    smem = pl.BlockSpec(memory_space=pltpu.SMEM)
    anywhere = pl.BlockSpec(memory_space=pl.ANY)
    return pl.pallas_call(
        functools.partial(spread_kernel, len(pieces), slots),
        out_shape=jax.ShapeDtypeStruct((tiles_side, features, side), jnp.float32),
        in_specs=[smem, smem, smem, anywhere, *([anywhere] * len(pieces))],
        out_specs=pl.BlockSpec(memory_space=pltpu.VMEM),
        scratch_shapes=[
            pltpu.VMEM(held, jnp.bfloat16),
            pltpu.VMEM(tiles.shape, jnp.bfloat16),
            pltpu.VMEM((tiles_side + 1, features, side), jnp.float32),
            pltpu.SemaphoreType.DMA((len(pieces),)),
            pltpu.SemaphoreType.DMA((blocks_total,)),
        ],
        compiler_params=pltpu.CompilerParams(vmem_limit_bytes=40 * 2**20),
        cost_estimate=pl.CostEstimate(
            flops=2 * blocks_total * slots * side * side * features,
            bytes_accessed=tiles.size * 2 + blocks_total * tiles_side * features * side * 2,
            transcendentals=0,
        ),
        name="spread",
    )(ids, rows, cols, tiles, *pieces)


def on_device(
    features, aggregated, out_grad, w_self, w_neigh, tiles, tile_rows, tile_cols, tile_counts
):
    block_total = lax.axis_size("blk")
    copies = lax.axis_size("rep")
    planes = block_total // PLANE
    block = lax.axis_index("blk")
    core = lax.rem(block, 2)
    plane = block // PLANE
    share_rows, width = out_grad.shape
    side = tiles.shape[-1]
    slots = tiles.shape[2]
    per_share = share_rows // side
    tiles_side = per_share * copies
    slice_width = width // copies
    member = PLANE * copies
    groups = [[p * member + m for m in range(member)] for p in range(planes)]

    share = lax.dot_general(
        w_neigh, out_grad, (((1,), (1,)), ((), ())), preferred_element_type=jnp.float32
    ).astype(jnp.bfloat16)
    share = share.reshape(copies, slice_width, per_share, side).swapaxes(1, 2)
    sent = jnp.broadcast_to(share, (PLANE, *share.shape)).reshape(member, *share.shape[1:])
    arrived = plane_exchange(sent, groups)
    own = arrived.reshape(PLANE, tiles_side, slice_width, side)

    contract = (((0,), (0,)), ((), ()))
    terms_self = lax.dot_general(features, out_grad, contract, preferred_element_type=jnp.float32)
    terms_neigh = lax.dot_general(
        aggregated, out_grad, contract, preferred_element_type=jnp.float32
    )
    stacked = jnp.concatenate([terms_self, terms_neigh], axis=0)
    part = plane_exchange(stacked.reshape(member, -1, width), groups).sum(axis=0)
    hop = 1
    while hop < planes:
        pairs = [(b, b ^ (PLANE * hop)) for b in range(block_total)]
        part = part + lax.ppermute(part, "blk", pairs)
        hop *= 2
    scale = (share_rows * block_total * copies) ** (-0.5)
    part = part * scale
    whole = plane_exchange(jnp.broadcast_to(part, (member, *part.shape)), groups)
    whole = whole.reshape(2 * width, width)

    onward = [
        (b, (b + PLANE) % block_total if b % 2 == 0 else (b - PLANE) % block_total)
        for b in range(block_total)
    ]
    partner = [(b, b ^ 1) for b in range(block_total)]
    back = 1 - 2 * core
    lanes = jnp.arange(PLANE, dtype=jnp.int32)
    moving = [own[m : m + 1] for m in range(PLANE)]
    got, got_ids = [], []
    for step in range(1, planes // 2):
        moving = [lax.ppermute(m, "blk", onward) for m in moving]
        got += moving
        got_ids.append(lax.rem(plane - back * step + planes, planes) * PLANE + lanes)
    half = PLANE // 2
    last = [
        lax.ppermute(jnp.where(core == 0, moving[m], moving[m + half]), "blk", onward)
        for m in range(half)
    ]
    got += last
    far = lax.rem(plane + planes // 2, planes) * PLANE
    got_ids.append(far + core * half + lanes[:half])
    swapped = [lax.ppermute(g, "blk", partner) for g in got]
    swapped_ids = [
        lax.rem(plane + back * step + planes, planes) * PLANE + lanes
        for step in range(1, planes // 2)
    ]
    swapped_ids.append(far + (1 - core) * half + lanes[:half])
    ids = jnp.concatenate([plane * PLANE + lanes, *got_ids, *swapped_ids])

    live = jnp.arange(slots, dtype=jnp.int32)[None, :] < tile_counts[0][:, None]
    rows = jnp.where(live, tile_rows[0], tiles_side).reshape(-1)
    cols = jnp.where(live, tile_cols[0], 0).reshape(-1)
    spread = spread_over([own, *got, *swapped], ids, rows, cols, tiles[0], tiles_side)

    parts = spread.reshape(copies, per_share, slice_width, side)
    parts = lax.all_to_all(parts, "rep", 0, 0, tiled=True)
    spread_share = parts.transpose(1, 3, 0, 2).reshape(share_rows, width)
    self_part = lax.dot_general(
        out_grad, w_self, (((1,), (1,)), ((), ())), preferred_element_type=jnp.float32
    )
    return (spread_share + self_part, whole[:width], whole[width:])


def solution(mesh):
    placed = (
        P(("blk", "rep"), None),
        P(("blk", "rep"), None),
        P(("blk", "rep"), None),
        P(),
        P(),
        P("blk", None, None, None, None),
        P("blk", None, None),
        P("blk", None, None),
        P("blk", None),
    )
    return jax.shard_map(
        on_device,
        mesh=mesh,
        in_specs=placed,
        out_specs=(P(("blk", "rep"), None), P(), P()),
        check_vma=False,
    )
```

```python
import functools

import jax
import jax.numpy as jnp
from jax import lax
from jax.experimental import pallas as pl
from jax.experimental.pallas import tpu as pltpu
from jax.sharding import PartitionSpec as P

PLANE = 4
HALF = PLANE // 2
BOTH = ("blk", "rep")
AS_SHORT = pl.CostEstimate(flops=1, bytes_accessed=0, transcendentals=0)
AS_LONG = pl.CostEstimate(flops=20000000000, bytes_accessed=0, transcendentals=0)
VMEM = pl.BlockSpec(memory_space=pltpu.VMEM)
SMEM = pl.BlockSpec(memory_space=pltpu.SMEM)
ROOM = pltpu.CompilerParams(vmem_limit_bytes=16 * 2**20)
BY_LAST = (((1,), (1,)), ((), ()))


def exchange(x, axes, groups=None):
    return lax.all_to_all(x, axes, 0, 0, axis_index_groups=groups, tiled=True)


def opening_kernel(features, aggregated, grad, weight, out):
    share = lax.dot_general(
        weight[...], grad[...], BY_LAST, preferred_element_type=jnp.float32
    ).astype(out.dtype)
    again, slices, held, width, side = out.shape
    tiles = held - 2
    for s in range(slices):
        for t in range(tiles):
            part = share[s * width : (s + 1) * width, t * side : (t + 1) * side]
            for q in range(again):
                out[q, s, t] = part
    depth = width // 2
    rows = slices * depth
    for q in range(again):
        source = (features, aggregated)[q // HALF]
        first = q % HALF * rows
        terms = lax.dot_general(
            source[:, first : first + rows],
            grad[...],
            (((0,), (0,)), ((), ())),
            preferred_element_type=jnp.float32,
        )
        upper = terms.astype(out.dtype)
        lower = (terms - upper.astype(jnp.float32)).astype(out.dtype)
        for s in range(slices):
            here = slice(s * depth, (s + 1) * depth)
            for place, half in ((tiles, upper), (tiles + 1, lower)):
                out[q, s, place, :depth] = half[here, :side]
                out[q, s, place, depth:] = half[here, side:]


def opening(features, aggregated, out_grad, w_neigh, copies, side):
    rows, width = out_grad.shape
    shape = (PLANE, copies, rows // side + 2, width // copies, side)
    return pl.pallas_call(
        opening_kernel,
        out_shape=jax.ShapeDtypeStruct(shape, jnp.bfloat16),
        compiler_params=pltpu.CompilerParams(vmem_limit_bytes=60 * 2**20),
        name="opening",
    )(features, aggregated, out_grad, w_neigh)


def plane_sum_kernel(arrived, out):
    tiles = arrived.shape[1] - 2
    total = jnp.zeros(out.shape[1:], jnp.float32)
    for m in range(arrived.shape[0]):
        total = total + (
            arrived[m, tiles].astype(jnp.float32) + arrived[m, tiles + 1].astype(jnp.float32)
        )
    for copy in range(out.shape[0]):
        out[copy] = total


def plane_sum(arrived, again):
    return pl.pallas_call(
        plane_sum_kernel,
        out_shape=jax.ShapeDtypeStruct((again, *arrived.shape[2:]), jnp.float32),
        compiler_params=ROOM,
        name="plane_sum",
    )(arrived)


def codes_kernel(tiles_side, rows, cols, counts, out):
    slot = lax.broadcasted_iota(jnp.int32, out.shape, 0)
    code = rows[0] * tiles_side + cols[0]
    out[...] = jnp.where(slot < counts[...], code, tiles_side * tiles_side)


def slot_codes(tile_rows, tile_cols, tile_counts, tiles_side):
    _, blocks, slots = tile_rows.shape
    return pl.pallas_call(
        functools.partial(codes_kernel, tiles_side),
        out_shape=jax.ShapeDtypeStruct((slots, blocks), jnp.int32),
        cost_estimate=AS_LONG,
        compiler_params=ROOM,
        name="codes",
    )(tile_rows.swapaxes(1, 2), tile_cols.swapaxes(1, 2), tile_counts)


def summed_kernel(scale, parts, out):
    total = parts[0]
    for p in range(1, parts.shape[0]):
        total = total + parts[p]
    if scale != 1.0:
        total = total * scale
    for copy in range(out.shape[0]):
        out[copy] = total


def summed(parts, again, scale):
    return pl.pallas_call(
        functools.partial(summed_kernel, scale),
        out_shape=jax.ShapeDtypeStruct((again, *parts.shape[1:]), parts.dtype),
        compiler_params=ROOM,
        name="summed",
    )(parts)


def result_kernel(parts, whole, grad, weight, out, self_out, neigh_out):
    straight = lax.dot_general(
        grad[...], weight[...], BY_LAST, preferred_element_type=jnp.float32
    )
    slices, tiles, width, side = parts.shape
    for t in range(tiles):
        rows = slice(t * side, (t + 1) * side)
        spread = parts[:, t].reshape(slices * width, side)
        out[rows] = straight[rows] + spread.T
    members, depth = whole.shape[0], whole.shape[1] // 2
    for m in range(members):
        target = (self_out, neigh_out)[2 * m // members]
        top = m % (members // 2) * depth
        target[top : top + depth, :side] = whole[m, :depth]
        target[top : top + depth, side:] = whole[m, depth:]


def result(parts, whole, out_grad, w_self):
    rows, width = out_grad.shape
    return pl.pallas_call(
        result_kernel,
        out_shape=[
            jax.ShapeDtypeStruct((rows, width), jnp.float32),
            jax.ShapeDtypeStruct((width, width), jnp.float32),
            jax.ShapeDtypeStruct((width, width), jnp.float32),
        ],
        compiler_params=ROOM,
        name="result",
    )(parts, whole, out_grad, w_self)


def spread_kernel(sources, resumed, codes, tiles, *refs):
    pieces, refs = refs[: len(sources)], refs[len(sources) :]
    begun, refs = (refs[0], refs[1:]) if resumed else (None, refs)
    out, acc = refs
    tiles_side, width, side = out.shape
    slots = tiles.shape[2]
    shift = tiles_side.bit_length() - 1
    block = lax.axis_index("blk")
    acc[:tiles_side] = begun[...] if resumed else jnp.zeros(out.shape, jnp.float32)
    acc[tiles_side] = jnp.zeros(out.shape[1:], jnp.float32)
    for piece, source_of in zip(pieces, sources):
        for m in range(piece.shape[0]):
            source = source_of(block, m)
            code = [codes[k, source] for k in range(slots)]
            row = [lax.shift_right_logical(c, shift) for c in code]
            col = [lax.bitwise_and(c, tiles_side - 1) for c in code]
            for k in range(0, slots, 2):
                pair = jnp.concatenate([piece[m, col[k]], piece[m, col[k + 1]]], axis=0)
                both = tiles[0, source, k : k + 2].reshape(2 * side, side)
                product = lax.dot_general(
                    pair, both, BY_LAST, preferred_element_type=jnp.float32
                )
                acc[row[k]] = acc[row[k]] + product[:width, :side]
                acc[row[k + 1]] = acc[row[k + 1]] + product[width:, side:]
    out[...] = acc[:tiles_side]


def spread_over(pieces, sources, codes, tiles, begun=None):
    _, tiles_side, width, side = pieces[0].shape
    shape = (tiles_side, width, side)
    resumed = begun is not None
    operands = [tiles, *pieces, *([begun] if resumed else [])]
    return pl.pallas_call(
        functools.partial(spread_kernel, sources, resumed),
        out_shape=jax.ShapeDtypeStruct(shape, jnp.float32),
        in_specs=[SMEM] + [VMEM] * len(operands),
        out_specs=VMEM,
        scratch_shapes=[pltpu.VMEM((tiles_side + 1, width, side), jnp.float32)],
        compiler_params=ROOM,
        cost_estimate=AS_SHORT if resumed else AS_LONG,
        name="spread_on" if resumed else "spread",
    )(codes, *operands)


def on_device(
    features, aggregated, out_grad, w_self, w_neigh, tiles, tile_rows, tile_cols, tile_counts
):
    block_total = lax.axis_size("blk")
    copies = lax.axis_size("rep")
    planes = block_total // PLANE
    core = lax.rem(lax.axis_index("blk"), 2)
    share_rows, width = out_grad.shape
    side = tiles.shape[-1]
    tiles_side = share_rows // side * copies
    member = PLANE * copies
    in_plane = [[p * member + m for m in range(member)] for p in range(planes)]
    over_planes = [[p * PLANE + q for p in range(planes)] for q in range(PLANE)]

    sent = opening(features, aggregated, out_grad, w_neigh, copies, side)
    arrived = exchange(sent.reshape(member, *sent.shape[2:]), BOTH, in_plane)
    own = arrived[:, :-2].reshape(PLANE, tiles_side, *sent.shape[3:])

    onward = [
        (b, (b + PLANE) % block_total if b % 2 == 0 else (b - PLANE) % block_total)
        for b in range(block_total)
    ]
    partner = [(b, b ^ 1) for b in range(block_total)]
    near = jnp.where(core == 0, own[:HALF], own[HALF:])
    other = jnp.where(core == 0, own[HALF:], own[:HALF])
    steps = planes // 2
    def source(step, flip, swap):
        def of(block, m):
            core = lax.rem(block, 2)
            core = 1 - core if swap else core
            away = jnp.where(core == 0, planes - step, step)
            plane = lax.rem(block // PLANE + away, planes)
            return plane * PLANE + (1 - core if flip else core) * HALF + m

        return of

    codes = slot_codes(tile_rows, tile_cols, tile_counts, tiles_side)

    def summed_on(total, *work):
        pieces = [p for p, *_ in work]
        return spread_over(pieces, [source(*w[1:]) for w in work], codes, tiles, total)

    scale = (share_rows * block_total * copies) ** (-0.5)
    part = plane_sum(arrived, planes)
    nears, others, swaps = [near], [other], [[]]
    total, waiting = None, []

    part = exchange(part, "blk", over_planes)
    for step in range(steps):
        near, other = nears[-1], others[-1]
        if step == 2:
            near, codes = lax.optimization_barrier((near, codes))
        if step == 2:
            near, part = lax.optimization_barrier((near, part))
            whole = exchange(summed(part, member, scale), BOTH, in_plane)
        nears[-1] = near
        nears.append(lax.ppermute(near, "blk", onward))
        if step < steps - 1:
            others.append(lax.ppermute(other, "blk", onward))
        waiting += [(near, step, False, False), (other, step, True, False)]
        if step == steps - 1:
            total = summed_on(None, *waiting)
            waiting = []
        if step > 0:
            waiting += [
                (lax.ppermute(near, "blk", partner), step, False, True),
                (lax.ppermute(other, "blk", partner), step, True, True),
            ]
    final, total = lax.optimization_barrier((nears[-1], total))
    last = (lax.ppermute(final, "blk", partner), steps, False, True)
    spread = summed_on(total, *waiting, (final, steps, False, False), last)
    spread, whole = lax.optimization_barrier((spread, whole))
    parts = exchange(spread.reshape(copies, -1, *spread.shape[1:]), "rep")
    return result(parts, whole, out_grad, w_self)


def solution(mesh):
    placed = (
        P(("blk", "rep"), None),
        P(("blk", "rep"), None),
        P(("blk", "rep"), None),
        P(),
        P(),
        P("blk", None, None, None, None),
        P("blk", None, None),
        P("blk", None, None),
        P("blk", None),
    )
    return jax.shard_map(
        on_device,
        mesh=mesh,
        in_specs=placed,
        out_specs=(P(("blk", "rep"), None), P(), P()),
        check_vma=False,
    )
```

```python
import functools

import jax
import jax.numpy as jnp
from jax import lax
from jax.experimental import pallas as pl
from jax.experimental.pallas import tpu as pltpu
from jax.sharding import PartitionSpec as P

PLANE = 4
HALF = PLANE // 2
LOW = 2
MEMBERS = 32
RUN = 4
TOGETHER = 4
BOTH = ("blk", "rep")
AS_SHORT = pl.CostEstimate(flops=1, bytes_accessed=0, transcendentals=0)
AS_LONG = pl.CostEstimate(flops=20000000000, bytes_accessed=0, transcendentals=0)
VMEM = pl.BlockSpec(memory_space=pltpu.VMEM)
SMEM = pl.BlockSpec(memory_space=pltpu.SMEM)
ROOM = pltpu.CompilerParams(vmem_limit_bytes=16 * 2**20)
BY_LAST = (((1,), (1,)), ((), ()))


def exchange(x, axes, groups=None):
    return lax.all_to_all(x, axes, 0, 0, axis_index_groups=groups, tiled=True)


def opening_kernel(features, aggregated, grad, weight, out):
    share = lax.dot_general(
        weight[...], grad[...], BY_LAST, preferred_element_type=jnp.float32
    ).astype(out.dtype)
    members, held, width, side = out.shape
    tiles = held - 2
    for p in range(members):
        s = slice_of(p)
        for t in range(tiles):
            out[p, t] = share[s * width : (s + 1) * width, t * side : (t + 1) * side]
    depth = width // 2
    half = members // 2
    for which, source in enumerate((features, aggregated)):
        terms = lax.dot_general(
            source[...], grad[...], (((0,), (0,)), ((), ())), preferred_element_type=jnp.float32
        )
        upper = terms.astype(out.dtype)
        lower = (terms - upper.astype(jnp.float32)).astype(out.dtype)
        for p in range(half):
            here = slice(p * depth, (p + 1) * depth)
            for place, part in ((tiles, upper), (tiles + 1, lower)):
                out[which * half + p, place, :depth] = part[here, :side]
                out[which * half + p, place, depth:] = part[here, side:]


def slice_of(p):
    return p // (HALF * LOW) % (MEMBERS // (PLANE * LOW)) * LOW + p % LOW


def opening(features, aggregated, out_grad, w_neigh, copies, side):
    rows, width = out_grad.shape
    shape = (PLANE * copies, rows // side + 2, width // copies, side)
    return pl.pallas_call(
        opening_kernel,
        out_shape=jax.ShapeDtypeStruct(shape, jnp.bfloat16),
        compiler_params=pltpu.CompilerParams(vmem_limit_bytes=60 * 2**20),
        name="opening",
    )(features, aggregated, out_grad, w_neigh)


def plane_sum_kernel(arrived, out):
    tiles = arrived.shape[1] - 2
    total = jnp.zeros(out.shape[1:], jnp.float32)
    for m in range(arrived.shape[0]):
        total = total + (
            arrived[m, tiles].astype(jnp.float32) + arrived[m, tiles + 1].astype(jnp.float32)
        )
    for copy in range(out.shape[0]):
        out[copy] = total


def plane_sum(arrived, again):
    return pl.pallas_call(
        plane_sum_kernel,
        out_shape=jax.ShapeDtypeStruct((again, *arrived.shape[2:]), jnp.float32),
        compiler_params=ROOM,
        name="plane_sum",
    )(arrived)


def codes_kernel(tiles_side, rows, cols, counts, out):
    slot = lax.broadcasted_iota(jnp.int32, out.shape, 0)
    code = rows[0] * tiles_side + cols[0]
    out[...] = jnp.where(slot < counts[...], code, tiles_side * tiles_side)


def slot_codes(tile_rows, tile_cols, tile_counts, tiles_side):
    _, blocks, slots = tile_rows.shape
    return pl.pallas_call(
        functools.partial(codes_kernel, tiles_side),
        out_shape=jax.ShapeDtypeStruct((slots, blocks), jnp.int32),
        cost_estimate=AS_LONG,
        compiler_params=ROOM,
        name="codes",
    )(tile_rows.swapaxes(1, 2), tile_cols.swapaxes(1, 2), tile_counts)


def summed_kernel(scale, parts, out):
    total = parts[0]
    for p in range(1, parts.shape[0]):
        total = total + parts[p]
    if scale != 1.0:
        total = total * scale
    for copy in range(out.shape[0]):
        out[copy] = total


def summed(parts, again, scale):
    return pl.pallas_call(
        functools.partial(summed_kernel, scale),
        out_shape=jax.ShapeDtypeStruct((again, *parts.shape[1:]), parts.dtype),
        compiler_params=ROOM,
        name="summed",
    )(parts)


def result_kernel(parts, whole, grad, weight, out, self_out, neigh_out):
    straight = lax.dot_general(
        grad[...], weight[...], BY_LAST, preferred_element_type=jnp.float32
    )
    slices, tiles, width, side = parts.shape
    for t in range(tiles):
        rows = slice(t * side, (t + 1) * side)
        spread = parts[:, t].reshape(slices * width, side)
        out[rows] = straight[rows] + spread.T
    members, depth = whole.shape[0], whole.shape[1] // 2
    for m in range(members):
        target = (self_out, neigh_out)[2 * m // members]
        top = m % (members // 2) * depth
        target[top : top + depth, :side] = whole[m, :depth]
        target[top : top + depth, side:] = whole[m, depth:]


def result(parts, whole, out_grad, w_self):
    rows, width = out_grad.shape
    return pl.pallas_call(
        result_kernel,
        out_shape=[
            jax.ShapeDtypeStruct((rows, width), jnp.float32),
            jax.ShapeDtypeStruct((width, width), jnp.float32),
            jax.ShapeDtypeStruct((width, width), jnp.float32),
        ],
        compiler_params=ROOM,
        name="result",
    )(parts, whole, out_grad, w_self)


def add_products(acc, codes, tiles, piece, source, m, shift):
    slots = tiles.shape[1]
    _, width, side = acc.shape
    code = [codes[k, source] for k in range(slots)]
    row = [lax.shift_right_logical(c, shift) for c in code]
    col = [lax.bitwise_and(c, (1 << shift) - 1) for c in code]
    at = [c + lax.bitwise_and(c, -RUN) + RUN * m for c in col]
    for k in range(0, slots, 2):
        pair = jnp.concatenate([piece[at[k]], piece[at[k + 1]]], axis=0)
        both = tiles[source, k : k + 2].reshape(2 * side, side)
        product = lax.dot_general(pair, both, BY_LAST, preferred_element_type=jnp.float32)
        acc[row[k]] = acc[row[k]] + product[:width, :side]
        acc[row[k + 1]] = acc[row[k + 1]] + product[width:, side:]


def spread_kernel(sources, later, codes, tiles, *refs):
    pieces, (out, held, acc, sems) = refs[: len(sources)], refs[len(sources) :]
    tiles_side = out.shape[0]
    shift = tiles_side.bit_length() - 1
    block = lax.axis_index("blk")
    work = [(p, of(block, m), m) for p, of in zip(pieces, sources) for m in range(HALF)]
    rest = [of(block, m) for of in later for m in range(HALF)]
    copies = [
        pltpu.make_async_copy(tiles.at[0, source], held.at[source], sems.at[n])
        for n, source in enumerate([source for _, source, _ in work] + rest)
    ]
    for copy in copies:
        copy.start()
    acc[...] = jnp.zeros_like(acc)
    for n in range(0, len(work), TOGETHER):
        for copy in copies[n : n + TOGETHER]:
            copy.wait()
        for piece, source, m in work[n : n + TOGETHER]:
            add_products(acc, codes, held, piece, source, m, shift)
    for copy in copies[len(work) :]:
        copy.wait()
    out[...] = acc[:tiles_side]


def spread_over(pieces, sources, later, codes, tiles, tiles_side):
    _, width, side = pieces[0].shape
    shape = (tiles_side, width, side)
    return pl.pallas_call(
        functools.partial(spread_kernel, sources, later),
        out_shape=[
            jax.ShapeDtypeStruct(shape, jnp.float32),
            jax.ShapeDtypeStruct(tiles.shape[1:], tiles.dtype),
        ],
        in_specs=[SMEM, pl.BlockSpec(memory_space=pltpu.HBM)] + [VMEM] * len(pieces),
        out_specs=[VMEM, VMEM],
        scratch_shapes=[
            pltpu.VMEM((tiles_side + 1, width, side), jnp.float32),
            pltpu.SemaphoreType.DMA((tiles.shape[1],)),
        ],
        compiler_params=pltpu.CompilerParams(vmem_limit_bytes=40 * 2**20),
        cost_estimate=AS_LONG,
        name="spread",
    )(codes, tiles, *pieces)


def spread_on_kernel(sources, codes, tiles, begun, *refs):
    pieces, (out, acc) = refs[: len(sources)], refs[len(sources) :]
    tiles_side = out.shape[0]
    block = lax.axis_index("blk")
    acc[:tiles_side] = begun[...]
    acc[tiles_side] = jnp.zeros(out.shape[1:], jnp.float32)
    for piece, of in zip(pieces, sources):
        for m in range(HALF):
            source = of(block, m)
            add_products(acc, codes, tiles, piece, source, m, tiles_side.bit_length() - 1)
    out[...] = acc[:tiles_side]


def spread_on(pieces, sources, codes, tiles, begun):
    return pl.pallas_call(
        functools.partial(spread_on_kernel, sources),
        out_shape=jax.ShapeDtypeStruct(begun.shape, jnp.float32),
        in_specs=[SMEM] + [VMEM] * (2 + len(pieces)),
        out_specs=VMEM,
        scratch_shapes=[pltpu.VMEM((begun.shape[0] + 1, *begun.shape[1:]), jnp.float32)],
        compiler_params=ROOM,
        cost_estimate=AS_SHORT,
        name="spread_on",
    )(codes, tiles, begun, *pieces)


def on_device(
    features, aggregated, out_grad, w_self, w_neigh, tiles, tile_rows, tile_cols, tile_counts
):
    block_total = lax.axis_size("blk")
    copies = lax.axis_size("rep")
    planes = block_total // PLANE
    core = lax.rem(lax.axis_index("blk"), 2)
    share_rows, width = out_grad.shape
    side = tiles.shape[-1]
    tiles_side = share_rows // side * copies
    member = PLANE * copies
    in_plane = [
        [
            ((z * HALF + high) * HALF + c) * copies + x * LOW + low
            for c in range(HALF)
            for x in range(copies // LOW)
            for high in range(HALF)
            for low in range(LOW)
        ]
        for z in range(planes)
    ]
    over_planes = [[p * PLANE + q for p in range(planes)] for q in range(PLANE)]

    sent = opening(features, aggregated, out_grad, w_neigh, copies, side)
    arrived = exchange(sent, BOTH, in_plane)
    own = arrived[:, :-2].reshape(2, member, *sent.shape[2:])

    onward = [
        (b, (b + PLANE) % block_total if b % 2 == 0 else (b - PLANE) % block_total)
        for b in range(block_total)
    ]
    partner = [(b, b ^ 1) for b in range(block_total)]
    near = jnp.where(core == 0, own[0], own[1])
    other = jnp.where(core == 0, own[1], own[0])
    steps = planes // 2
    def source(step, flip, swap):
        def of(block, m):
            core = lax.rem(block, 2)
            core = 1 - core if swap else core
            away = jnp.where(core == 0, planes - step, step)
            plane = lax.rem(block // PLANE + away, planes)
            return plane * PLANE + m * HALF + (1 - core if flip else core)

        return of

    codes = slot_codes(tile_rows, tile_cols, tile_counts, tiles_side)

    scale = (share_rows * block_total * copies) ** (-0.5)
    part = plane_sum(arrived, planes)
    nears, others, swaps = [near], [other], [[]]
    part = exchange(part, "blk", over_planes)
    swaps = []
    for step in range(steps):
        near, other = nears[-1], others[-1]
        if step == 2:
            near, codes, part = lax.optimization_barrier((near, codes, part))
            whole = exchange(summed(part, member, scale), BOTH, in_plane)
        nears[-1] = near
        nears.append(lax.ppermute(near, "blk", onward))
        if step < steps - 1:
            others.append(lax.ppermute(other, "blk", onward))
        if step > 0:
            swaps += [
                (lax.ppermute(near, "blk", partner), source(step, False, True)),
                (lax.ppermute(other, "blk", partner), source(step, True, True)),
            ]
    early = [(p, source(s, False, False)) for s, p in enumerate(nears[:-1])]
    early += [(p, source(s, True, False)) for s, p in enumerate(others)]
    later = [of for _, of in swaps] + [source(steps, False, swap) for swap in (False, True)]
    total, held = spread_over(*zip(*early), later, codes, tiles, tiles_side)
    final, total = lax.optimization_barrier((nears[-1], total))
    late = [p for p, _ in swaps] + [final, lax.ppermute(final, "blk", partner)]
    spread = spread_on(late, later, codes, held, total)
    spread, whole = lax.optimization_barrier((spread, whole))
    parts = exchange(spread.reshape(copies, -1, *spread.shape[1:]), "rep")
    return result(parts, whole, out_grad, w_self)


def solution(mesh):
    placed = (
        P(("blk", "rep"), None),
        P(("blk", "rep"), None),
        P(("blk", "rep"), None),
        P(),
        P(),
        P("blk", None, None, None, None),
        P("blk", None, None),
        P("blk", None, None),
        P("blk", None),
    )
    return jax.shard_map(
        on_device,
        mesh=mesh,
        in_specs=placed,
        out_specs=(P(("blk", "rep"), None), P(), P()),
        check_vma=False,
    )
```

```python
import functools

import jax
import jax.numpy as jnp
from jax import lax
from jax.experimental import pallas as pl
from jax.experimental.pallas import tpu as pltpu
from jax.sharding import PartitionSpec as P

PLANE = 4
HALF = PLANE // 2
LOW = 2
MEMBERS = 32
RUN = 4
TOGETHER = 4
BOTH = ("blk", "rep")
AS_A_HOP = pl.CostEstimate(flops=100000000, bytes_accessed=0, transcendentals=0)
AS_SHORT = pl.CostEstimate(flops=1, bytes_accessed=0, transcendentals=0)
AS_LONG = pl.CostEstimate(flops=20000000000, bytes_accessed=0, transcendentals=0)
VMEM = pl.BlockSpec(memory_space=pltpu.VMEM)
SMEM = pl.BlockSpec(memory_space=pltpu.SMEM)
ROOM = pltpu.CompilerParams(vmem_limit_bytes=16 * 2**20)
BY_LAST = (((1,), (1,)), ((), ()))


def exchange(x, axes, groups=None):
    return lax.all_to_all(x, axes, 0, 0, axis_index_groups=groups, tiled=True)


def opening_kernel(features, aggregated, grad, weight, out):
    share = lax.dot_general(
        weight[...], grad[...], BY_LAST, preferred_element_type=jnp.float32
    ).astype(out.dtype)
    members, held, width, side = out.shape
    tiles = held - 4
    for p in range(members):
        s = slice_of(p)
        for t in range(tiles):
            out[p, t] = share[s * width : (s + 1) * width, t * side : (t + 1) * side]
    depth = width // 2
    for which, source in enumerate((features, aggregated)):
        terms = lax.dot_general(
            source[...], grad[...], (((0,), (0,)), ((), ())), preferred_element_type=jnp.float32
        )
        upper = terms.astype(out.dtype)
        lower = (terms - upper.astype(jnp.float32)).astype(out.dtype)
        for p in range(members):
            here = slice(p * depth, (p + 1) * depth)
            for place, part in enumerate((upper, lower), tiles + 2 * which):
                out[p, place, :depth] = part[here, :side]
                out[p, place, depth:] = part[here, side:]


def slice_of(p):
    return p // (HALF * LOW) % (MEMBERS // (PLANE * LOW)) * LOW + p % LOW


def opening(features, aggregated, out_grad, w_neigh, copies, side):
    rows, width = out_grad.shape
    shape = (HALF * copies, rows // side + 4, width // copies, side)
    return pl.pallas_call(
        opening_kernel,
        out_shape=jax.ShapeDtypeStruct(shape, jnp.bfloat16),
        compiler_params=pltpu.CompilerParams(vmem_limit_bytes=60 * 2**20),
        name="opening",
    )(features, aggregated, out_grad, w_neigh)


def half_sums_kernel(arrived, keep, give):
    members, held, _, _ = arrived.shape
    core = lax.rem(lax.axis_index("blk"), 2)
    sums = []
    for first in range(held - 4, held, 2):
        total = jnp.zeros(keep.shape, jnp.float32)
        for m in range(members):
            total = total + (
                arrived[m, first].astype(jnp.float32) + arrived[m, first + 1].astype(jnp.float32)
            )
        sums.append(total)
    keep[...] = jnp.where(core == 0, sums[0], sums[1])
    give[...] = jnp.where(core == 0, sums[1], sums[0])


def half_sums(arrived):
    shape = jax.ShapeDtypeStruct(arrived.shape[2:], jnp.float32)
    return pl.pallas_call(
        half_sums_kernel,
        out_shape=[shape, shape],
        compiler_params=ROOM,
        name="half_sums",
    )(arrived)


def joined_kernel(keep, got, out):
    total = keep[...] + got[...]
    for copy in range(out.shape[0]):
        out[copy] = total


def joined(keep, got, again):
    return pl.pallas_call(
        joined_kernel,
        out_shape=jax.ShapeDtypeStruct((again, *keep.shape), keep.dtype),
        compiler_params=ROOM,
        name="joined",
    )(keep, got)


def gate_kernel(block, before, out):
    out[...] = jnp.zeros_like(out)


def gate(block, before):
    anywhere = pl.BlockSpec(memory_space=pl.ANY)
    return pl.pallas_call(
        gate_kernel,
        out_shape=jax.ShapeDtypeStruct((8, 128), jnp.int32),
        in_specs=[anywhere, anywhere],
        compiler_params=ROOM,
        cost_estimate=AS_A_HOP,
        name="gate",
    )(block, before)


def codes_kernel(tiles_side, rows, cols, counts, out):
    slot = lax.broadcasted_iota(jnp.int32, out.shape, 0)
    code = rows[0] * tiles_side + cols[0]
    out[...] = jnp.where(slot < counts[...], code, tiles_side * tiles_side)


def slot_codes(tile_rows, tile_cols, tile_counts, tiles_side):
    _, blocks, slots = tile_rows.shape
    return pl.pallas_call(
        functools.partial(codes_kernel, tiles_side),
        out_shape=jax.ShapeDtypeStruct((slots, blocks), jnp.int32),
        cost_estimate=AS_LONG,
        compiler_params=ROOM,
        name="codes",
    )(tile_rows.swapaxes(1, 2), tile_cols.swapaxes(1, 2), tile_counts)


def summed_kernel(scale, parts, out):
    total = parts[0]
    for p in range(1, parts.shape[0]):
        total = total + parts[p]
    if scale != 1.0:
        total = total * scale
    for copy in range(out.shape[0]):
        out[copy] = total


def summed(parts, again, scale):
    return pl.pallas_call(
        functools.partial(summed_kernel, scale),
        out_shape=jax.ShapeDtypeStruct((again, *parts.shape[1:]), parts.dtype),
        compiler_params=ROOM,
        name="summed",
    )(parts)


def result_kernel(parts, whole, grad, weight, token, out, self_out, neigh_out):
    straight = lax.dot_general(
        grad[...], weight[...], BY_LAST, preferred_element_type=jnp.float32
    )
    slices, tiles, width, side = parts.shape
    for t in range(tiles):
        rows = slice(t * side, (t + 1) * side)
        spread = parts[:, t].reshape(slices * width, side)
        out[rows] = straight[rows] + spread.T
    members, depth = whole.shape[0], whole.shape[1] // 2
    for m in range(members):
        target = (self_out, neigh_out)[2 * m // members]
        top = m % (members // 2) * depth
        target[top : top + depth, :side] = whole[m, :depth]
        target[top : top + depth, side:] = whole[m, depth:]


def result(parts, whole, out_grad, w_self, token):
    rows, width = out_grad.shape
    return pl.pallas_call(
        result_kernel,
        out_shape=[
            jax.ShapeDtypeStruct((rows, width), jnp.float32),
            jax.ShapeDtypeStruct((width, width), jnp.float32),
            jax.ShapeDtypeStruct((width, width), jnp.float32),
        ],
        compiler_params=ROOM,
        name="result",
    )(parts, whole, out_grad, w_self, token)


def add_products(acc, codes, tiles, piece, source, m, shift):
    slots = tiles.shape[1]
    _, width, side = acc.shape
    code = [codes[k, source] for k in range(slots)]
    row = [lax.shift_right_logical(c, shift) for c in code]
    col = [lax.bitwise_and(c, (1 << shift) - 1) for c in code]
    at = [c + lax.bitwise_and(c, -RUN) + RUN * m for c in col]
    for k in range(0, slots, 2):
        pair = jnp.concatenate([piece[at[k]], piece[at[k + 1]]], axis=0)
        both = tiles[source, k : k + 2].reshape(2 * side, side)
        product = lax.dot_general(pair, both, BY_LAST, preferred_element_type=jnp.float32)
        acc[row[k]] = acc[row[k]] + product[:width, :side]
        acc[row[k + 1]] = acc[row[k + 1]] + product[width:, side:]


def spread_kernel(sources, later, codes, tiles, *refs):
    pieces, (out, held, acc, sems) = refs[: len(sources)], refs[len(sources) :]
    tiles_side = out.shape[0]
    shift = tiles_side.bit_length() - 1
    block = lax.axis_index("blk")
    work = [(p, of(block, m), m) for p, of in zip(pieces, sources) for m in range(HALF)]
    rest = [of(block, m) for of in later for m in range(HALF)]
    copies = [
        pltpu.make_async_copy(tiles.at[0, source], held.at[source], sems.at[n])
        for n, source in enumerate([source for _, source, _ in work] + rest)
    ]
    for copy in copies:
        copy.start()
    acc[...] = jnp.zeros_like(acc)
    for n in range(0, len(work), TOGETHER):
        for copy in copies[n : min(n + TOGETHER, len(work))]:
            copy.wait()
        for piece, source, m in work[n : n + TOGETHER]:
            add_products(acc, codes, held, piece, source, m, shift)
    for copy in copies[len(work) :]:
        copy.wait()
    out[...] = acc[:tiles_side]


def spread_over(pieces, sources, later, codes, tiles, tiles_side):
    _, width, side = pieces[0].shape
    shape = (tiles_side, width, side)
    return pl.pallas_call(
        functools.partial(spread_kernel, sources, later),
        out_shape=[
            jax.ShapeDtypeStruct(shape, jnp.float32),
            jax.ShapeDtypeStruct(tiles.shape[1:], tiles.dtype),
        ],
        in_specs=[SMEM, pl.BlockSpec(memory_space=pltpu.HBM)] + [VMEM] * len(pieces),
        out_specs=[VMEM, VMEM],
        scratch_shapes=[
            pltpu.VMEM((tiles_side + 1, width, side), jnp.float32),
            pltpu.SemaphoreType.DMA((tiles.shape[1],)),
        ],
        compiler_params=pltpu.CompilerParams(vmem_limit_bytes=40 * 2**20),
        cost_estimate=AS_LONG,
        name="spread",
    )(codes, tiles, *pieces)


def spread_on_kernel(sources, codes, tiles, begun, *refs):
    pieces, (out, acc) = refs[: len(sources)], refs[len(sources) :]
    tiles_side = out.shape[0]
    block = lax.axis_index("blk")
    acc[:tiles_side] = begun[...]
    acc[tiles_side] = jnp.zeros(out.shape[1:], jnp.float32)
    for piece, of in zip(pieces, sources):
        for m in range(HALF):
            source = of(block, m)
            add_products(acc, codes, tiles, piece, source, m, tiles_side.bit_length() - 1)
    out[...] = acc[:tiles_side]


def spread_on(pieces, sources, codes, tiles, begun):
    return pl.pallas_call(
        functools.partial(spread_on_kernel, sources),
        out_shape=jax.ShapeDtypeStruct(begun.shape, jnp.float32),
        in_specs=[SMEM] + [VMEM] * (2 + len(pieces)),
        out_specs=VMEM,
        scratch_shapes=[pltpu.VMEM((begun.shape[0] + 1, *begun.shape[1:]), jnp.float32)],
        compiler_params=ROOM,
        cost_estimate=AS_SHORT,
        name="spread_on",
    )(codes, tiles, begun, *pieces)


def on_device(
    features, aggregated, out_grad, w_self, w_neigh, tiles, tile_rows, tile_cols, tile_counts
):
    block_total = lax.axis_size("blk")
    copies = lax.axis_size("rep")
    planes = block_total // PLANE
    share_rows, width = out_grad.shape
    side = tiles.shape[-1]
    tiles_side = share_rows // side * copies
    member = PLANE * copies
    in_plane = [
        [
            ((z * HALF + high) * HALF + c) * copies + x * LOW + low
            for c in range(HALF)
            for x in range(copies // LOW)
            for high in range(HALF)
            for low in range(LOW)
        ]
        for z in range(planes)
    ]
    over_planes = [[p * PLANE + q for p in range(planes)] for q in range(PLANE)]

    sent = opening(features, aggregated, out_grad, w_neigh, copies, side)
    half = member // HALF
    arrived = exchange(sent, BOTH, [g[c * half :][:half] for g in in_plane for c in range(HALF)])

    onward = [
        (b, (b + PLANE) % block_total if b % 2 == 0 else (b - PLANE) % block_total)
        for b in range(block_total)
    ]
    partner = [(b, b ^ 1) for b in range(block_total)]
    near = arrived[:, :-4].reshape(member, *sent.shape[2:])
    other = lax.ppermute(near, "blk", partner)
    steps = planes // 2
    def source(step, flip, swap):
        def of(block, m):
            core = lax.rem(block, 2)
            core = 1 - core if swap else core
            away = jnp.where(core == 0, planes - step, step)
            plane = lax.rem(block // PLANE + away, planes)
            return plane * PLANE + m * HALF + (1 - core if flip else core)

        return of

    codes = slot_codes(tile_rows, tile_cols, tile_counts, tiles_side)

    scale = (share_rows * block_total * copies) ** (-0.5)
    keep, give = half_sums(arrived)
    given = lax.ppermute(give, "blk", partner)
    nears, others = [near], [other]
    swaps, token = [], None
    part = exchange(joined(keep, given, planes), "blk", over_planes)
    for step in range(steps):
        near, other = nears[-1], others[-1]
        if step == 2:
            near, codes, part = lax.optimization_barrier((near, codes, part))
            whole = exchange(summed(part, member, scale), BOTH, in_plane)
            token = codes
        if step > 2:
            near, token = lax.optimization_barrier((near, token))
        nears[-1] = near
        nears.append(lax.ppermute(near, "blk", onward))
        if step >= 2:
            token = gate(near, token)
            other, token = lax.optimization_barrier((other, token))
            others[-1] = other
        if step > 0:
            swaps += [
                (lax.ppermute(near, "blk", partner), source(step, False, True)),
                (lax.ppermute(other, "blk", partner), source(step, True, True)),
            ]
        if step < steps - 1:
            others.append(lax.ppermute(other, "blk", onward))
            if step >= 2:
                token = gate(other, token)
    early = [(p, source(s, False, False)) for s, p in enumerate(nears[:-1])]
    early += [(p, source(s, True, False)) for s, p in enumerate(others[:-1])]
    middle = [(others[-1], source(steps - 1, True, False)), *swaps]
    ends = [source(steps, False, False), source(steps, False, True)]
    later = [of for _, of in middle] + ends
    total, held = spread_over(*zip(*early), later, codes, tiles, tiles_side)
    total = spread_on(*zip(*middle), codes, held, total)
    final, total = lax.optimization_barrier((nears[-1], total))
    late = [final, lax.ppermute(final, "blk", partner)]
    spread = spread_on(late, ends, codes, held, total)
    spread, whole = lax.optimization_barrier((spread, whole))
    parts = exchange(spread.reshape(copies, -1, *spread.shape[1:]), "rep")
    return result(parts, whole, out_grad, w_self, token)


def solution(mesh):
    placed = (
        P(("blk", "rep"), None),
        P(("blk", "rep"), None),
        P(("blk", "rep"), None),
        P(),
        P(),
        P("blk", None, None, None, None),
        P("blk", None, None),
        P("blk", None, None),
        P("blk", None),
    )
    return jax.shard_map(
        on_device,
        mesh=mesh,
        in_specs=placed,
        out_specs=(P(("blk", "rep"), None), P(), P()),
        check_vma=False,
    )
```

```python
import functools

import jax
import jax.numpy as jnp
from jax import lax
from jax.experimental import pallas as pl
from jax.experimental.pallas import tpu as pltpu
from jax.sharding import PartitionSpec as P

PLANE = 4
HALF = PLANE // 2
LOW = 2
MEMBERS = 32
RUN = 4
TOGETHER = 4
BOTH = ("blk", "rep")
AS_A_HOP = pl.CostEstimate(flops=100000000, bytes_accessed=0, transcendentals=0)
AS_SHORT = pl.CostEstimate(flops=1, bytes_accessed=0, transcendentals=0)
AS_LONG = pl.CostEstimate(flops=20000000000, bytes_accessed=0, transcendentals=0)
VMEM = pl.BlockSpec(memory_space=pltpu.VMEM)
SMEM = pl.BlockSpec(memory_space=pltpu.SMEM)
ROOM = pltpu.CompilerParams(vmem_limit_bytes=16 * 2**20)
BY_LAST = (((1,), (1,)), ((), ()))


def exchange(x, axes, groups=None):
    return lax.all_to_all(x, axes, 0, 0, axis_index_groups=groups, tiled=True)


def opening_kernel(features, aggregated, grad, weight, out):
    share = lax.dot_general(
        weight[...], grad[...], BY_LAST, preferred_element_type=jnp.float32
    ).astype(out.dtype)
    members, held, width, side = out.shape
    tiles = held - 4
    for p in range(members):
        s = slice_of(p)
        for t in range(tiles):
            out[p, t] = share[s * width : (s + 1) * width, t * side : (t + 1) * side]
    depth = width // 2
    for which, source in enumerate((features, aggregated)):
        terms = lax.dot_general(
            source[...], grad[...], (((0,), (0,)), ((), ())), preferred_element_type=jnp.float32
        )
        upper = terms.astype(out.dtype)
        lower = (terms - upper.astype(jnp.float32)).astype(out.dtype)
        for p in range(members):
            here = slice(p * depth, (p + 1) * depth)
            for place, part in enumerate((upper, lower), tiles + 2 * which):
                out[p, place, :depth] = part[here, :side]
                out[p, place, depth:] = part[here, side:]


def slice_of(p):
    return p // (HALF * LOW) % (MEMBERS // (PLANE * LOW)) * LOW + p % LOW


def opening(features, aggregated, out_grad, w_neigh, copies, side):
    rows, width = out_grad.shape
    shape = (HALF * copies, rows // side + 4, width // copies, side)
    return pl.pallas_call(
        opening_kernel,
        out_shape=jax.ShapeDtypeStruct(shape, jnp.bfloat16),
        compiler_params=pltpu.CompilerParams(vmem_limit_bytes=60 * 2**20),
        name="opening",
    )(features, aggregated, out_grad, w_neigh)


def half_sums_kernel(arrived, keep, give):
    members, held, _, _ = arrived.shape
    core = lax.rem(lax.axis_index("blk"), 2)
    sums = []
    for first in range(held - 4, held, 2):
        total = jnp.zeros(keep.shape, jnp.float32)
        for m in range(members):
            total = total + (
                arrived[m, first].astype(jnp.float32) + arrived[m, first + 1].astype(jnp.float32)
            )
        sums.append(total)
    keep[...] = jnp.where(core == 0, sums[0], sums[1])
    give[...] = jnp.where(core == 0, sums[1], sums[0])


def half_sums(arrived):
    shape = jax.ShapeDtypeStruct(arrived.shape[2:], jnp.float32)
    return pl.pallas_call(
        half_sums_kernel,
        out_shape=[shape, shape],
        compiler_params=ROOM,
        name="half_sums",
    )(arrived)


def joined_kernel(keep, got, out):
    total = keep[...] + got[...]
    for copy in range(out.shape[0]):
        out[copy] = total


def joined(keep, got, again):
    return pl.pallas_call(
        joined_kernel,
        out_shape=jax.ShapeDtypeStruct((again, *keep.shape), keep.dtype),
        compiler_params=ROOM,
        name="joined",
    )(keep, got)


def gate_kernel(block, before, out):
    out[...] = jnp.zeros_like(out)


def gate(block, before):
    anywhere = pl.BlockSpec(memory_space=pl.ANY)
    return pl.pallas_call(
        gate_kernel,
        out_shape=jax.ShapeDtypeStruct((8, 128), jnp.int32),
        in_specs=[anywhere, anywhere],
        compiler_params=ROOM,
        cost_estimate=AS_A_HOP,
        name="gate",
    )(block, before)


def codes_kernel(tiles_side, rows, cols, counts, out):
    slot = lax.broadcasted_iota(jnp.int32, out.shape, 0)
    code = rows[0] * tiles_side + cols[0]
    out[...] = jnp.where(slot < counts[...], code, tiles_side * tiles_side)


def slot_codes(tile_rows, tile_cols, tile_counts, tiles_side):
    _, blocks, slots = tile_rows.shape
    return pl.pallas_call(
        functools.partial(codes_kernel, tiles_side),
        out_shape=jax.ShapeDtypeStruct((slots, blocks), jnp.int32),
        cost_estimate=AS_LONG,
        compiler_params=ROOM,
        name="codes",
    )(tile_rows.swapaxes(1, 2), tile_cols.swapaxes(1, 2), tile_counts)


def summed_kernel(scale, parts, out):
    total = parts[0]
    for p in range(1, parts.shape[0]):
        total = total + parts[p]
    if scale != 1.0:
        total = total * scale
    for copy in range(out.shape[0]):
        out[copy] = total


def summed(parts, again, scale):
    return pl.pallas_call(
        functools.partial(summed_kernel, scale),
        out_shape=jax.ShapeDtypeStruct((again, *parts.shape[1:]), parts.dtype),
        compiler_params=ROOM,
        name="summed",
    )(parts)


def result_kernel(parts, whole, grad, weight, token, out, self_out, neigh_out):
    straight = lax.dot_general(
        grad[...], weight[...], BY_LAST, preferred_element_type=jnp.float32
    )
    slices, tiles, width, side = parts.shape
    for t in range(tiles):
        rows = slice(t * side, (t + 1) * side)
        spread = parts[:, t].reshape(slices * width, side)
        out[rows] = straight[rows] + spread.T
    members, depth = whole.shape[0], whole.shape[1] // 2
    for m in range(members):
        target = (self_out, neigh_out)[2 * m // members]
        top = m % (members // 2) * depth
        target[top : top + depth, :side] = whole[m, :depth]
        target[top : top + depth, side:] = whole[m, depth:]


def result(parts, whole, out_grad, w_self, token):
    rows, width = out_grad.shape
    return pl.pallas_call(
        result_kernel,
        out_shape=[
            jax.ShapeDtypeStruct((rows, width), jnp.float32),
            jax.ShapeDtypeStruct((width, width), jnp.float32),
            jax.ShapeDtypeStruct((width, width), jnp.float32),
        ],
        compiler_params=ROOM,
        name="result",
    )(parts, whole, out_grad, w_self, token)


def add_products(acc, codes, tiles, piece, source, m, shift):
    slots = tiles.shape[1]
    _, width, side = acc.shape
    code = [codes[k, source] for k in range(slots)]
    row = [lax.shift_right_logical(c, shift) for c in code]
    col = [lax.bitwise_and(c, (1 << shift) - 1) for c in code]
    at = [c + lax.bitwise_and(c, -RUN) + RUN * m for c in col]
    for k in range(0, slots, 2):
        pair = jnp.concatenate([piece[at[k]], piece[at[k + 1]]], axis=0)
        both = tiles[source, k : k + 2].reshape(2 * side, side)
        product = lax.dot_general(pair, both, BY_LAST, preferred_element_type=jnp.float32)
        acc[row[k]] = acc[row[k]] + product[:width, :side]
        acc[row[k + 1]] = acc[row[k + 1]] + product[width:, side:]


def spread_kernel(sources, later, codes, tiles, *refs):
    pieces, (out, held, acc, sems) = refs[: len(sources)], refs[len(sources) :]
    tiles_side = out.shape[0]
    shift = tiles_side.bit_length() - 1
    block = lax.axis_index("blk")
    work = [(p, of(block, m), m) for p, of in zip(pieces, sources) for m in range(HALF)]
    rest = [of(block, m) for of in later for m in range(HALF)]
    copies = [
        pltpu.make_async_copy(tiles.at[0, source], held.at[source], sems.at[n])
        for n, source in enumerate([source for _, source, _ in work] + rest)
    ]
    for copy in copies:
        copy.start()
    acc[...] = jnp.zeros_like(acc)
    for n in range(0, len(work), TOGETHER):
        for copy in copies[n : min(n + TOGETHER, len(work))]:
            copy.wait()
        for piece, source, m in work[n : n + TOGETHER]:
            add_products(acc, codes, held, piece, source, m, shift)
    for copy in copies[len(work) :]:
        copy.wait()
    out[...] = acc[:tiles_side]


def spread_over(pieces, sources, later, codes, tiles, tiles_side):
    _, width, side = pieces[0].shape
    shape = (tiles_side, width, side)
    return pl.pallas_call(
        functools.partial(spread_kernel, sources, later),
        out_shape=[
            jax.ShapeDtypeStruct(shape, jnp.float32),
            jax.ShapeDtypeStruct(tiles.shape[1:], tiles.dtype),
        ],
        in_specs=[SMEM, pl.BlockSpec(memory_space=pltpu.HBM)] + [VMEM] * len(pieces),
        out_specs=[VMEM, VMEM],
        scratch_shapes=[
            pltpu.VMEM((tiles_side + 1, width, side), jnp.float32),
            pltpu.SemaphoreType.DMA((tiles.shape[1],)),
        ],
        compiler_params=pltpu.CompilerParams(vmem_limit_bytes=40 * 2**20),
        cost_estimate=AS_LONG,
        name="spread",
    )(codes, tiles, *pieces)


def spread_on_kernel(sources, codes, tiles, begun, *refs):
    pieces, (out, acc) = refs[: len(sources)], refs[len(sources) :]
    tiles_side = out.shape[0]
    block = lax.axis_index("blk")
    acc[:tiles_side] = begun[...]
    acc[tiles_side] = jnp.zeros(out.shape[1:], jnp.float32)
    for piece, of in zip(pieces, sources):
        for m in range(HALF):
            source = of(block, m)
            add_products(acc, codes, tiles, piece, source, m, tiles_side.bit_length() - 1)
    out[...] = acc[:tiles_side]


def spread_on(pieces, sources, codes, tiles, begun):
    return pl.pallas_call(
        functools.partial(spread_on_kernel, sources),
        out_shape=jax.ShapeDtypeStruct(begun.shape, jnp.float32),
        in_specs=[SMEM] + [VMEM] * (2 + len(pieces)),
        out_specs=VMEM,
        scratch_shapes=[pltpu.VMEM((begun.shape[0] + 1, *begun.shape[1:]), jnp.float32)],
        compiler_params=ROOM,
        cost_estimate=AS_SHORT,
        name="spread_on",
    )(codes, tiles, begun, *pieces)


def on_device(
    features, aggregated, out_grad, w_self, w_neigh, tiles, tile_rows, tile_cols, tile_counts
):
    block_total = lax.axis_size("blk")
    copies = lax.axis_size("rep")
    planes = block_total // PLANE
    share_rows, width = out_grad.shape
    side = tiles.shape[-1]
    tiles_side = share_rows // side * copies
    member = PLANE * copies
    in_plane = [
        [
            ((z * HALF + high) * HALF + c) * copies + x * LOW + low
            for c in range(HALF)
            for x in range(copies // LOW)
            for high in range(HALF)
            for low in range(LOW)
        ]
        for z in range(planes)
    ]
    over_planes = [[p * PLANE + q for p in range(planes)] for q in range(PLANE)]

    sent = opening(features, aggregated, out_grad, w_neigh, copies, side)
    half = member // HALF
    arrived = exchange(sent, BOTH, [g[c * half :][:half] for g in in_plane for c in range(HALF)])

    onward = [
        (b, (b + PLANE) % block_total if b % 2 == 0 else (b - PLANE) % block_total)
        for b in range(block_total)
    ]
    partner = [(b, b ^ 1) for b in range(block_total)]
    near = arrived[:, :-4].reshape(member, *sent.shape[2:])
    other = lax.ppermute(near, "blk", partner)
    steps = planes // 2
    def source(step, flip, swap):
        def of(block, m):
            core = lax.rem(block, 2)
            core = 1 - core if swap else core
            away = jnp.where(core == 0, planes - step, step)
            plane = lax.rem(block // PLANE + away, planes)
            return plane * PLANE + m * HALF + (1 - core if flip else core)

        return of

    codes = slot_codes(tile_rows, tile_cols, tile_counts, tiles_side)

    scale = (share_rows * block_total * copies) ** (-0.5)
    keep, give = half_sums(arrived)
    given = lax.ppermute(give, "blk", partner)
    near, given = lax.optimization_barrier((near, given))
    nears, others = [near], [other]
    swaps, token = [], None
    part = exchange(joined(keep, given, planes), "blk", over_planes)
    for step in range(steps):
        near, other = nears[-1], others[-1]
        if step == 2:
            near, codes, part = lax.optimization_barrier((near, codes, part))
            whole = exchange(summed(part, member, scale), BOTH, in_plane)
            token = codes
        if step > 2:
            near, token = lax.optimization_barrier((near, token))
        nears[-1] = near
        nears.append(lax.ppermute(near, "blk", onward))
        if step >= 2:
            token = gate(near, token)
            other, token = lax.optimization_barrier((other, token))
            others[-1] = other
        if step > 0:
            swaps += [
                (lax.ppermute(near, "blk", partner), source(step, False, True)),
                (lax.ppermute(other, "blk", partner), source(step, True, True)),
            ]
        if step < steps - 1:
            others.append(lax.ppermute(other, "blk", onward))
            if step >= 2:
                token = gate(other, token)
    early = [(p, source(s, False, False)) for s, p in enumerate(nears[:-1])]
    early += [(p, source(s, True, False)) for s, p in enumerate(others[:-1])]
    middle = [(others[-1], source(steps - 1, True, False)), *swaps]
    ends = [source(steps, False, False), source(steps, False, True)]
    later = [of for _, of in middle] + ends
    total, held = spread_over(*zip(*early), later, codes, tiles, tiles_side)
    total = spread_on(*zip(*middle), codes, held, total)
    final, total = lax.optimization_barrier((nears[-1], total))
    late = [final, lax.ppermute(final, "blk", partner)]
    spread = spread_on(late, ends, codes, held, total)
    spread, whole = lax.optimization_barrier((spread, whole))
    parts = exchange(spread.reshape(copies, -1, *spread.shape[1:]), "rep")
    return result(parts, whole, out_grad, w_self, token)


def solution(mesh):
    placed = (
        P(("blk", "rep"), None),
        P(("blk", "rep"), None),
        P(("blk", "rep"), None),
        P(),
        P(),
        P("blk", None, None, None, None),
        P("blk", None, None),
        P("blk", None, None),
        P("blk", None),
    )
    return jax.shard_map(
        on_device,
        mesh=mesh,
        in_specs=placed,
        out_specs=(P(("blk", "rep"), None), P(), P()),
        check_vma=False,
    )
```

```python
import functools

import jax
import jax.numpy as jnp
from jax import lax
from jax.experimental import pallas as pl
from jax.experimental.pallas import tpu as pltpu
from jax.sharding import PartitionSpec as P

PLANE = 4
HALF = PLANE // 2
LOW = 2
MEMBERS = 32
RUN = 4
TOGETHER = 7
BOTH = ("blk", "rep")
AS_A_HOP = pl.CostEstimate(flops=100000000, bytes_accessed=0, transcendentals=0)
AS_SHORT = pl.CostEstimate(flops=1, bytes_accessed=0, transcendentals=0)
AS_LONG = pl.CostEstimate(flops=20000000000, bytes_accessed=0, transcendentals=0)
VMEM = pl.BlockSpec(memory_space=pltpu.VMEM)
SMEM = pl.BlockSpec(memory_space=pltpu.SMEM)
ROOM = pltpu.CompilerParams(vmem_limit_bytes=16 * 2**20)
BY_LAST = (((1,), (1,)), ((), ()))


def exchange(x, axes, groups=None):
    return lax.all_to_all(x, axes, 0, 0, axis_index_groups=groups, tiled=True)


def opening_kernel(features, aggregated, grad, weight, out):
    share = lax.dot_general(
        weight[...], grad[...], BY_LAST, preferred_element_type=jnp.float32
    ).astype(out.dtype)
    members, held, width, side = out.shape
    tiles = held - 4
    for p in range(members):
        s = slice_of(p)
        for t in range(tiles):
            out[p, t] = share[s * width : (s + 1) * width, t * side : (t + 1) * side]
    depth = width // 2
    for which, source in enumerate((features, aggregated)):
        terms = lax.dot_general(
            source[...], grad[...], (((0,), (0,)), ((), ())), preferred_element_type=jnp.float32
        )
        upper = terms.astype(out.dtype)
        lower = (terms - upper.astype(jnp.float32)).astype(out.dtype)
        for p in range(members):
            here = slice(p * depth, (p + 1) * depth)
            for place, part in enumerate((upper, lower), tiles + 2 * which):
                out[p, place, :depth] = part[here, :side]
                out[p, place, depth:] = part[here, side:]


def slice_of(p):
    return p // (HALF * LOW) % (MEMBERS // (PLANE * LOW)) * LOW + p % LOW


def opening(features, aggregated, out_grad, w_neigh, copies, side):
    rows, width = out_grad.shape
    shape = (HALF * copies, rows // side + 4, width // copies, side)
    return pl.pallas_call(
        opening_kernel,
        out_shape=jax.ShapeDtypeStruct(shape, jnp.bfloat16),
        compiler_params=pltpu.CompilerParams(vmem_limit_bytes=60 * 2**20),
        name="opening",
    )(features, aggregated, out_grad, w_neigh)


def half_sums_kernel(arrived, keep, give):
    members, held, _, _ = arrived.shape
    core = lax.rem(lax.axis_index("blk"), 2)
    sums = []
    for first in range(held - 4, held, 2):
        total = jnp.zeros(keep.shape, jnp.float32)
        for m in range(members):
            total = total + (
                arrived[m, first].astype(jnp.float32) + arrived[m, first + 1].astype(jnp.float32)
            )
        sums.append(total)
    keep[...] = jnp.where(core == 0, sums[0], sums[1])
    give[...] = jnp.where(core == 0, sums[1], sums[0])


def half_sums(arrived):
    shape = jax.ShapeDtypeStruct(arrived.shape[2:], jnp.float32)
    return pl.pallas_call(
        half_sums_kernel,
        out_shape=[shape, shape],
        compiler_params=ROOM,
        name="half_sums",
    )(arrived)


def joined_kernel(keep, got, out):
    total = keep[...] + got[...]
    for copy in range(out.shape[0]):
        out[copy] = total


def joined(keep, got, again):
    return pl.pallas_call(
        joined_kernel,
        out_shape=jax.ShapeDtypeStruct((again, *keep.shape), keep.dtype),
        compiler_params=ROOM,
        name="joined",
    )(keep, got)


def gate_kernel(block, before, out):
    out[...] = jnp.zeros_like(out)


def gate(block, before):
    anywhere = pl.BlockSpec(memory_space=pl.ANY)
    return pl.pallas_call(
        gate_kernel,
        out_shape=jax.ShapeDtypeStruct((8, 128), jnp.int32),
        in_specs=[anywhere, anywhere],
        compiler_params=ROOM,
        cost_estimate=AS_A_HOP,
        name="gate",
    )(block, before)


def codes_kernel(tiles_side, rows, cols, counts, out):
    slot = lax.broadcasted_iota(jnp.int32, out.shape, 0)
    code = rows[0] * tiles_side + cols[0]
    out[...] = jnp.where(slot < counts[...], code, tiles_side * tiles_side)


def slot_codes(tile_rows, tile_cols, tile_counts, tiles_side):
    _, blocks, slots = tile_rows.shape
    return pl.pallas_call(
        functools.partial(codes_kernel, tiles_side),
        out_shape=jax.ShapeDtypeStruct((slots, blocks), jnp.int32),
        cost_estimate=AS_LONG,
        compiler_params=ROOM,
        name="codes",
    )(tile_rows.swapaxes(1, 2), tile_cols.swapaxes(1, 2), tile_counts)


def summed_kernel(scale, parts, out):
    total = parts[0]
    for p in range(1, parts.shape[0]):
        total = total + parts[p]
    if scale != 1.0:
        total = total * scale
    for copy in range(out.shape[0]):
        out[copy] = total


def summed(parts, again, scale):
    return pl.pallas_call(
        functools.partial(summed_kernel, scale),
        out_shape=jax.ShapeDtypeStruct((again, *parts.shape[1:]), parts.dtype),
        compiler_params=ROOM,
        name="summed",
    )(parts)


def result_kernel(parts, whole, grad, weight, token, out, self_out, neigh_out):
    straight = lax.dot_general(
        grad[...], weight[...], BY_LAST, preferred_element_type=jnp.float32
    )
    slices, tiles, width, side = parts.shape
    for t in range(tiles):
        rows = slice(t * side, (t + 1) * side)
        spread = parts[:, t].reshape(slices * width, side)
        out[rows] = straight[rows] + spread.T
    members, depth = whole.shape[0], whole.shape[1] // 2
    for m in range(members):
        target = (self_out, neigh_out)[2 * m // members]
        top = m % (members // 2) * depth
        target[top : top + depth, :side] = whole[m, :depth]
        target[top : top + depth, side:] = whole[m, depth:]


def result(parts, whole, out_grad, w_self, token):
    rows, width = out_grad.shape
    return pl.pallas_call(
        result_kernel,
        out_shape=[
            jax.ShapeDtypeStruct((rows, width), jnp.float32),
            jax.ShapeDtypeStruct((width, width), jnp.float32),
            jax.ShapeDtypeStruct((width, width), jnp.float32),
        ],
        compiler_params=ROOM,
        name="result",
    )(parts, whole, out_grad, w_self, token)


def add_products(acc, codes, tiles, piece, source, m, shift):
    slots = tiles.shape[1]
    _, width, side = acc.shape
    code = [codes[k, source] for k in range(slots)]
    row = [lax.shift_right_logical(c, shift) for c in code]
    col = [lax.bitwise_and(c, (1 << shift) - 1) for c in code]
    at = [c + lax.bitwise_and(c, -RUN) + RUN * m for c in col]
    for k in range(0, slots, 2):
        pair = jnp.concatenate([piece[at[k]], piece[at[k + 1]]], axis=0)
        both = tiles[source, k : k + 2].reshape(2 * side, side)
        product = lax.dot_general(pair, both, BY_LAST, preferred_element_type=jnp.float32)
        acc[row[k]] = acc[row[k]] + product[:width, :side]
        acc[row[k + 1]] = acc[row[k + 1]] + product[width:, side:]


def spread_kernel(sources, later, codes, tiles, *refs):
    pieces, (out, held, acc, sems) = refs[: len(sources)], refs[len(sources) :]
    tiles_side = out.shape[0]
    shift = tiles_side.bit_length() - 1
    block = lax.axis_index("blk")
    work = [(p, of(block, m), m) for p, of in zip(pieces, sources) for m in range(HALF)]
    rest = [of(block, m) for of in later for m in range(HALF)]
    copies = [
        pltpu.make_async_copy(tiles.at[0, source], held.at[source], sems.at[n])
        for n, source in enumerate([source for _, source, _ in work] + rest)
    ]
    for copy in copies:
        copy.start()
    acc[...] = jnp.zeros_like(acc)
    for n in range(0, len(work), TOGETHER):
        for copy in copies[n : min(n + TOGETHER, len(work))]:
            copy.wait()
        for piece, source, m in work[n : n + TOGETHER]:
            add_products(acc, codes, held, piece, source, m, shift)
    for copy in copies[len(work) :]:
        copy.wait()
    out[...] = acc[:tiles_side]


def spread_over(pieces, sources, later, codes, tiles, tiles_side):
    _, width, side = pieces[0].shape
    shape = (tiles_side, width, side)
    return pl.pallas_call(
        functools.partial(spread_kernel, sources, later),
        out_shape=[
            jax.ShapeDtypeStruct(shape, jnp.float32),
            jax.ShapeDtypeStruct(tiles.shape[1:], tiles.dtype),
        ],
        in_specs=[SMEM, pl.BlockSpec(memory_space=pltpu.HBM)] + [VMEM] * len(pieces),
        out_specs=[VMEM, VMEM],
        scratch_shapes=[
            pltpu.VMEM((tiles_side + 1, width, side), jnp.float32),
            pltpu.SemaphoreType.DMA((tiles.shape[1],)),
        ],
        compiler_params=pltpu.CompilerParams(vmem_limit_bytes=40 * 2**20),
        cost_estimate=AS_LONG,
        name="spread",
    )(codes, tiles, *pieces)


def spread_on_kernel(sources, codes, tiles, begun, *refs):
    pieces, (out, acc) = refs[: len(sources)], refs[len(sources) :]
    tiles_side = out.shape[0]
    block = lax.axis_index("blk")
    acc[:tiles_side] = begun[...]
    acc[tiles_side] = jnp.zeros(out.shape[1:], jnp.float32)
    for piece, of in zip(pieces, sources):
        for m in range(HALF):
            source = of(block, m)
            add_products(acc, codes, tiles, piece, source, m, tiles_side.bit_length() - 1)
    out[...] = acc[:tiles_side]


def spread_on(pieces, sources, codes, tiles, begun):
    return pl.pallas_call(
        functools.partial(spread_on_kernel, sources),
        out_shape=jax.ShapeDtypeStruct(begun.shape, jnp.float32),
        in_specs=[SMEM] + [VMEM] * (2 + len(pieces)),
        out_specs=VMEM,
        scratch_shapes=[pltpu.VMEM((begun.shape[0] + 1, *begun.shape[1:]), jnp.float32)],
        compiler_params=ROOM,
        cost_estimate=AS_SHORT,
        name="spread_on",
    )(codes, tiles, begun, *pieces)


def on_device(
    features, aggregated, out_grad, w_self, w_neigh, tiles, tile_rows, tile_cols, tile_counts
):
    block_total = lax.axis_size("blk")
    copies = lax.axis_size("rep")
    planes = block_total // PLANE
    share_rows, width = out_grad.shape
    side = tiles.shape[-1]
    tiles_side = share_rows // side * copies
    member = PLANE * copies
    in_plane = [
        [
            ((z * HALF + high) * HALF + c) * copies + x * LOW + low
            for c in range(HALF)
            for x in range(copies // LOW)
            for high in range(HALF)
            for low in range(LOW)
        ]
        for z in range(planes)
    ]
    over_planes = [[p * PLANE + q for p in range(planes)] for q in range(PLANE)]

    sent = opening(features, aggregated, out_grad, w_neigh, copies, side)
    half = member // HALF
    arrived = exchange(sent, BOTH, [g[c * half :][:half] for g in in_plane for c in range(HALF)])

    onward = [
        (b, (b + PLANE) % block_total if b % 2 == 0 else (b - PLANE) % block_total)
        for b in range(block_total)
    ]
    partner = [(b, b ^ 1) for b in range(block_total)]
    near = arrived[:, :-4].reshape(member, *sent.shape[2:])
    other = lax.ppermute(near, "blk", partner)
    steps = planes // 2
    def source(step, flip, swap):
        def of(block, m):
            core = lax.rem(block, 2)
            core = 1 - core if swap else core
            away = jnp.where(core == 0, planes - step, step)
            plane = lax.rem(block // PLANE + away, planes)
            return plane * PLANE + m * HALF + (1 - core if flip else core)

        return of

    codes = slot_codes(tile_rows, tile_cols, tile_counts, tiles_side)

    scale = (share_rows * block_total * copies) ** (-0.5)
    keep, give = half_sums(arrived)
    given = lax.ppermute(give, "blk", partner)
    part = joined(keep, given, planes)
    near, other, part = lax.optimization_barrier((near, other, part))
    nears, others = [near], [other]
    swaps, token = [], None
    part = exchange(part, "blk", over_planes)
    for step in range(steps):
        near, other = nears[-1], others[-1]
        if step == 2:
            near, codes, part = lax.optimization_barrier((near, codes, part))
            whole = exchange(summed(part, member, scale), BOTH, in_plane)
            token = codes
        if step > 2:
            near, token = lax.optimization_barrier((near, token))
        nears[-1] = near
        nears.append(lax.ppermute(near, "blk", onward))
        if step >= 2:
            token = gate(near, token)
            other, token = lax.optimization_barrier((other, token))
            others[-1] = other
        if step > 0:
            swaps += [
                (lax.ppermute(near, "blk", partner), source(step, False, True)),
                (lax.ppermute(other, "blk", partner), source(step, True, True)),
            ]
        if step < steps - 1:
            others.append(lax.ppermute(other, "blk", onward))
            if step >= 2:
                token = gate(other, token)
    early = [(p, source(s, False, False)) for s, p in enumerate(nears[:-1])]
    early += [(p, source(s, True, False)) for s, p in enumerate(others[:-1])]
    middle = [(others[-1], source(steps - 1, True, False)), *swaps]
    ends = [source(steps, False, False), source(steps, False, True)]
    later = [of for _, of in middle] + ends
    total, held = spread_over(*zip(*early), later, codes, tiles, tiles_side)
    total = spread_on(*zip(*middle), codes, held, total)
    final, total = lax.optimization_barrier((nears[-1], total))
    late = [final, lax.ppermute(final, "blk", partner)]
    spread = spread_on(late, ends, codes, held, total)
    spread, whole = lax.optimization_barrier((spread, whole))
    parts = exchange(spread.reshape(copies, -1, *spread.shape[1:]), "rep")
    return result(parts, whole, out_grad, w_self, token)


def solution(mesh):
    placed = (
        P(("blk", "rep"), None),
        P(("blk", "rep"), None),
        P(("blk", "rep"), None),
        P(),
        P(),
        P("blk", None, None, None, None),
        P("blk", None, None),
        P("blk", None, None),
        P("blk", None),
    )
    return jax.shard_map(
        on_device,
        mesh=mesh,
        in_specs=placed,
        out_specs=(P(("blk", "rep"), None), P(), P()),
        check_vma=False,
    )
```
